128 devices in a mesh: comp: 2 (over z_hi), mr: 64 (over z_lo, y, x, core).
Axes of the slice: x: 4, y: 4, z: 4 (z_hi: 2, z_lo: 2; z = z_hi * 2 + z_lo), core: 2. Of those that a mesh axis runs over, the one named last changes fastest.
Arguments:
- spectrum: float32 [2, 1024, 2, 64, 512], P('comp', 'mr'), may hold values from -6 to 6
- radial_basis: bfloat16 [1024, 1024, 512], P('mr'), may hold values from -0.25 to 0.25
- cutoff: int32 [1024], P('mr'), may hold values from 128 to 512, as said below
- couplings: float32 [2, 2], replicated, may hold values from 0.5 to 1.5
- trap_potential: float32 [1024], replicated, may hold values from 0 to 2
- weights: float32 [1024], replicated, may hold values from 0.25 to 0.75
Outputs:
- evolved: float32 [2, 1024, 2, 64, 512], P('comp', 'mr')
The draws below stay inside these ranges and needn't reach their ends.
Inputs may be any that keep to these rules, and one draw needn't show every extreme that they name: cutoff[m] is the number of Laguerre degrees kept for angular mode m; degrees from cutoff[m] on are dropped.
All inputs are finite; a program needn't handle non-finite values.
Results may differ from the reference program's by a relative error of at most 0.0089.
Values may be sent and summed in bfloat16 or wider, within the bound.
A program may use at most 128 MiB of HBM per device.

```python
import math
import jax
import jax.numpy as jnp
from jax import lax

M = 1024
R = 1024
NL = 512
Z = 64


def draw_cutoff(key, part):
    positions = jnp.arange(M, dtype=jnp.int32)
    signed = jnp.where(positions < M // 2, positions, positions - M)
    magnitude = jnp.abs(signed).astype(jnp.int32)
    sloped = NL - magnitude * (NL // 2) // (M // 2)
    jitter = jax.random.randint(key, (M,), 0, max(NL // 8, 1), dtype=jnp.int32)
    values = sloped - jitter
    values = jnp.where(magnitude == 0, NL, values)
    values = jnp.where(magnitude == M // 2, NL // 4, values)
    return values.astype(jnp.int32)


def block_scale(key, dims, split, least, high):
    def one(axis_at, blocks):
        draws = jax.random.uniform(jax.random.fold_in(jax.random.fold_in(key, 6), axis_at), (blocks,), jnp.float32, least / len(split), high / len(split))
        return jnp.repeat(jnp.exp(draws), dims[axis_at] // blocks).reshape((-1,) + (1,) * (len(dims) - axis_at - 1))

    level = one(*split[0])
    for cut in split[1:]:
        level = level * one(*cut)
    return level


def normal_values(key, shape, spread, limit, cuts=(), kind=jnp.bfloat16):
    gain = block_scale(key, shape, cuts, -0.22, 0.18) if cuts else 1.0
    entries = jax.random.normal(key, shape, jnp.float32) * spread * gain
    return jnp.minimum(jnp.maximum(entries, -limit), limit).astype(kind)


def setup_inputs(seed: int = 0) -> dict:
    arg_keys = jax.random.split(jax.random.key(seed), 7)
    return {
        "spectrum": normal_values(arg_keys[0], (2, M, 2, Z, NL), 1.0, 6.0, ((0, 2), (1, 64)), jnp.float32),
        "radial_basis": normal_values(arg_keys[1], (M, R, NL), NL ** -0.5, 0.25, ((0, 64),)),
        "cutoff": draw_cutoff(jax.random.fold_in(arg_keys[6], 71), 0),
        "couplings": jnp.clip(jax.random.uniform(arg_keys[3], (2, 2), jnp.float32, 0.5, 1.5), 0.5, 1.5),
        "trap_potential": jnp.clip(jax.random.uniform(arg_keys[4], (R,), jnp.float32, 0.0, 2.0), 0.0, 2.0),
        "weights": jnp.clip(jax.random.uniform(arg_keys[5], (R,), jnp.float32, 0.25, 0.75), 0.25, 0.75),
    }


TIMESTEP = 0.5
ROTATION = 0.7

def spectral_tables(mode_total):
    ordinal = jnp.arange(mode_total, dtype=jnp.int32)
    product = ordinal[:, None] * ordinal[None, :] % mode_total
    angles = product.astype(jnp.float32) * (2.0 * math.pi / mode_total)
    normalizer = 1.0 / math.sqrt(mode_total)
    return ((jnp.cos(angles) * normalizer).astype(jnp.bfloat16), (jnp.sin(angles) * normalizer).astype(jnp.bfloat16))

def rotate(real_part, imag_part, phase_angle):
    cosine = jnp.cos(phase_angle)
    sine_value = jnp.sin(phase_angle)
    return (real_part * cosine + imag_part * sine_value, imag_part * cosine - real_part * sine_value)

def reference(spectrum, radial_basis, cutoff, couplings, trap_potential, weights):
    mode_ids = jnp.arange(M, dtype=jnp.int32)
    signed = jnp.where(mode_ids < M // 2, mode_ids, mode_ids - M).astype(jnp.float32)
    degree_ids = jnp.arange(NL, dtype=jnp.int32)
    energy = 2.0 * degree_ids.astype(jnp.float32)[None, :] + (jnp.abs(signed) + 1.0 - ROTATION * signed)[:, None]
    kinetic_phase = TIMESTEP * energy
    kept_mask = (degree_ids[None, :] < cutoff[:, None]).astype(jnp.float32)
    spin_real, spin_imag = rotate(spectrum[:, :, 0], spectrum[:, :, 1], kinetic_phase[None, :, None, :])
    coeffs = (jnp.stack([spin_real, spin_imag], 2) * kept_mask[None, :, None, None, :]).astype(jnp.bfloat16)
    per_mode = coeffs.transpose(1, 0, 2, 3, 4).reshape(M, 4 * Z, NL)

    def synthesize(operands):
        return jnp.dot(operands[0], operands[1].T, preferred_element_type=jnp.float32).astype(jnp.bfloat16)
    radial = lax.map(synthesize, (per_mode, radial_basis))
    block_count = 8
    block_rows = R // block_count
    blocks = radial.reshape(M, 4 * Z, block_count, block_rows).transpose(2, 0, 1, 3)
    cosine_table, sine_table = spectral_tables(M)

    def physical(operands):
        block_field, trap_rows, weight_rows = operands
        flattened = block_field.reshape(M, 4 * Z * block_rows)
        cosine_term = jnp.dot(cosine_table, flattened, preferred_element_type=jnp.float32).reshape(M, 2, 2, Z, block_rows)
        sine_term = jnp.dot(sine_table, flattened, preferred_element_type=jnp.float32).reshape(M, 2, 2, Z, block_rows)
        real_part = cosine_term[:, :, 0] - sine_term[:, :, 1]
        imag_part = sine_term[:, :, 0] + cosine_term[:, :, 1]
        density = real_part * real_part + imag_part * imag_part
        partner = density[:, ::-1]
        phase_angle = TIMESTEP * (couplings[:, 0][None, :, None, None] * density + couplings[:, 1][None, :, None, None] * partner + trap_rows[None, None, None, :])
        kick_real, kick_imag = rotate(real_part, imag_part, phase_angle)
        kicked = jnp.stack([kick_real, kick_imag], 2).astype(jnp.bfloat16).reshape(M, 4 * Z * block_rows)
        cosine_back = jnp.dot(cosine_table.T, kicked, preferred_element_type=jnp.float32).reshape(M, 2, 2, Z, block_rows)
        sine_back = jnp.dot(sine_table.T, kicked, preferred_element_type=jnp.float32).reshape(M, 2, 2, Z, block_rows)
        back_real = cosine_back[:, :, 0] + sine_back[:, :, 1]
        back_imag = cosine_back[:, :, 1] - sine_back[:, :, 0]
        weighted = jnp.stack([back_real, back_imag], 2) * weight_rows
        return weighted.astype(jnp.bfloat16).reshape(M, 4 * Z, block_rows)
    returned = lax.map(physical, (blocks, trap_potential.reshape(block_count, block_rows), weights.reshape(block_count, block_rows)))
    returned = returned.transpose(1, 2, 0, 3).reshape(M, 4 * Z, R)

    def analyze(operands):
        return jnp.dot(operands[0], operands[1], preferred_element_type=jnp.float32)
    evolved = lax.map(analyze, (returned, radial_basis)).reshape(M, 2, 2, Z, NL) * kept_mask[:, None, None, None, :]
    return evolved.transpose(1, 0, 2, 3, 4)
```

```python
import math

import jax
import jax.numpy as jnp
from jax import lax
from jax.sharding import PartitionSpec as P

TIMESTEP = 0.5
ROTATION = 0.7


def spectral_tables(mode_total):
    ordinal = jnp.arange(mode_total, dtype=jnp.int32)
    product = ordinal[:, None] * ordinal[None, :] % mode_total
    angles = product.astype(jnp.float32) * (2.0 * math.pi / mode_total)
    normalizer = 1.0 / math.sqrt(mode_total)
    return (
        (jnp.cos(angles) * normalizer).astype(jnp.bfloat16),
        (jnp.sin(angles) * normalizer).astype(jnp.bfloat16),
    )


def rotate(real_part, imag_part, phase_angle):
    cosine = jnp.cos(phase_angle)
    sine_value = jnp.sin(phase_angle)
    return (
        real_part * cosine + imag_part * sine_value,
        imag_part * cosine - real_part * sine_value,
    )


def forward_modes(cosine_table, sine_table, radial, planes):
    cosine_term = jnp.einsum(
        "am,rmk->rak", cosine_table, radial, preferred_element_type=jnp.float32
    )
    sine_term = jnp.einsum("am,rmk->rak", sine_table, radial, preferred_element_type=jnp.float32)
    real_part = cosine_term[..., :planes] - sine_term[..., planes:]
    imag_part = sine_term[..., :planes] + cosine_term[..., planes:]
    return (real_part, imag_part)


def inverse_modes(cosine_table, sine_table, kicked, planes):
    cosine_back = jnp.einsum(
        "am,rak->rmk", cosine_table, kicked, preferred_element_type=jnp.float32
    )
    sine_back = jnp.einsum("am,rak->rmk", sine_table, kicked, preferred_element_type=jnp.float32)
    back_real = cosine_back[..., :planes] + sine_back[..., planes:]
    back_imag = cosine_back[..., planes:] - sine_back[..., :planes]
    return jnp.concatenate([back_real, back_imag], -1)


def on_device(spectrum, radial_basis, cutoff, couplings, trap_potential, weights):
    local_modes = spectrum.shape[1]
    planes = spectrum.shape[3]
    degrees = spectrum.shape[4]
    radius_count = radial_basis.shape[1]
    mode_width = lax.axis_size("mr")
    mode_total = local_modes * mode_width
    first_mode = lax.axis_index("mr") * local_modes
    mode_ids = first_mode + jnp.arange(local_modes, dtype=jnp.int32)
    signed = jnp.where(mode_ids < mode_total // 2, mode_ids, mode_ids - mode_total).astype(
        jnp.float32
    )
    degree_ids = jnp.arange(degrees, dtype=jnp.int32)
    energy = (
        2.0 * degree_ids.astype(jnp.float32)[None, :]
        + (jnp.abs(signed) + 1.0 - ROTATION * signed)[:, None]
    )
    kinetic_phase = TIMESTEP * energy
    kept_mask = (degree_ids[None, :] < cutoff[:, None]).astype(jnp.float32)
    spin_real, spin_imag = rotate(spectrum[0, :, 0], spectrum[0, :, 1], kinetic_phase[:, None, :])
    coeffs = jnp.concatenate(
        [spin_real * kept_mask[:, None, :], spin_imag * kept_mask[:, None, :]], axis=1
    ).astype(jnp.bfloat16)
    synthesized = jnp.einsum(
        "mkn,mrn->rmk", coeffs, radial_basis, preferred_element_type=jnp.float32
    ).astype(jnp.bfloat16)
    cosine_table, sine_table = spectral_tables(mode_total)
    comp_width = lax.axis_size("comp")
    row_count = radius_count // (mode_width * comp_width)
    first_row = (lax.axis_index("comp") * mode_width + lax.axis_index("mr")) * row_count
    trap_rows = lax.dynamic_slice_in_dim(trap_potential, first_row, row_count)
    weight_rows = lax.dynamic_slice_in_dim(weights, first_row, row_count)
    everyone = ("comp", "mr")
    radial = lax.all_to_all(synthesized, everyone, split_axis=0, concat_axis=1, tiled=True)
    radial = radial.reshape(row_count * comp_width, mode_total, 2 * planes)
    real_part, imag_part = forward_modes(cosine_table, sine_table, radial, planes)
    density = (real_part * real_part + imag_part * imag_part).reshape(
        row_count, comp_width, mode_total, planes
    )
    phase_angle = TIMESTEP * (
        couplings[:, 0][None, :, None, None] * density
        + couplings[:, 1][None, :, None, None] * density[:, ::-1]
        + trap_rows[:, None, None, None]
    )
    kick_real, kick_imag = rotate(real_part, imag_part, phase_angle.reshape(real_part.shape))
    kicked = jnp.concatenate([kick_real, kick_imag], -1).astype(jnp.bfloat16)
    back = inverse_modes(cosine_table, sine_table, kicked, planes)
    back = back.reshape(row_count, comp_width * mode_total, 2 * planes)
    analysis_input = (back * weight_rows[:, None, None]).astype(jnp.bfloat16)
    gathered_modes = lax.all_to_all(
        analysis_input, everyone, split_axis=1, concat_axis=0, tiled=True
    )
    evolved = (
        jnp.einsum("rmk,mrn->mkn", gathered_modes, radial_basis, preferred_element_type=jnp.float32)
        * kept_mask[:, None, :]
    )
    return evolved.reshape(1, local_modes, 2, planes, degrees)


def solution(mesh):
    in_specs = (P("comp", "mr", None, None, None), P("mr", None, None), P("mr"), P(), P(), P())
    out_specs = P("comp", "mr", None, None, None)
    return jax.shard_map(
        on_device, mesh=mesh, in_specs=in_specs, out_specs=out_specs, check_vma=False
    )
```

```python
import functools
import math

import jax
import jax.numpy as jnp
import ml_dtypes
import numpy as np
from jax import lax
from jax.experimental import pallas as pl
from jax.experimental.pallas import tpu as pltpu
from jax.sharding import PartitionSpec as P

TIMESTEP = 0.5
ROTATION = 0.7
MESH = pl.DeviceIdType.MESH
CHUNKS = 4
GROUPS = 4
QUARTERS = 4
F32 = jnp.float32
BF16 = jnp.bfloat16


def quarter_tables(mode_total):
    quarter = mode_total // QUARTERS
    angle = QUARTERS * np.arange(quarter)[None, :, None] + np.arange(QUARTERS)[:, None, None]
    product = angle * np.arange(quarter)[None, None, :] % mode_total
    turn = product * (2.0 * math.pi / mode_total)
    both = np.stack([np.cos(turn), np.sin(turn)], 1) / math.sqrt(mode_total)
    both = both.astype(np.float32).astype(ml_dtypes.bfloat16)
    return np.stack([both, both.swapaxes(-1, -2)])


def sine_cosine(angle):
    turns = jnp.round(angle * (2.0 / math.pi))
    rest = angle - turns * 1.5703125
    rest = rest - turns * 4.837512969970703125e-4
    rest = rest - turns * 7.54978995489188e-8
    rest = jnp.clip(rest, -0.8, 0.8)
    square = rest * rest
    sine = ((-1.9515295891e-4 * square + 8.3321608736e-3) * square - 1.6666654611e-1) * square
    sine = sine * rest + rest
    cosine = (2.443315711809948e-5 * square - 1.388731625493765e-3) * square
    cosine = (cosine + 4.166664568298827e-2) * square * square - 0.5 * square + 1.0
    corner = (turns - 4.0 * jnp.floor(turns * 0.25)).astype(jnp.int32)
    swap = (corner & 1) == 1
    sine, cosine = jnp.where(swap, cosine, sine), jnp.where(swap, sine, cosine)
    sine = jnp.where(corner >= 2, -sine, sine)
    cosine = jnp.where((corner == 1) | (corner == 2), -cosine, cosine)
    return sine, cosine


def sine_cosine_of_turns(turns):
    rest = turns - jnp.round(turns)
    square = rest * rest
    twice = 0.1553153206018442 * square - 1.1965825712357152
    twice = (twice * square + 5.100155046428268) * square - 10.335420167015725
    twice = (twice * square + 6.283185280261414) * rest
    cosine = 0.2196896110917421 * square - 1.3318765680776314
    cosine = (cosine * square + 4.058411352862034) * square - 4.93479283061961
    cosine = cosine * square + 0.9999999532476082
    return twice * cosine, 1.0 - 0.5 * (twice * twice)


def kernel(
    cutoff_hbm, couplings_hbm, trap_hbm, weights_hbm, spectrum_hbm, basis_hbm, tables_hbm, total,
    basis, coeffs, tables, forward, inverse, sent, landed, sent_back, landed_back,
    stage, turned, field, kicked, modes, wave_cos, wave_sin,
    cutoff, couplings, trap, weights, load_sem, scalar_sem, spectrum_sem, first_sem, basis_sem, send_sem, recv_sem, send_back_sem, recv_back_sem,
):
    comps, group = lax.axis_size("comp"), lax.axis_size("mr")
    comp, place = lax.axis_index("comp"), lax.axis_index("mr")
    devices = comps * group
    me = comp * group + place
    local = coeffs.shape[0]
    planes = coeffs.shape[1] // 2
    degrees = coeffs.shape[2]
    rows = basis.shape[2]
    half = rows // 2
    quarter = forward.shape[1] // 2
    quarter_places = group // QUARTERS
    mode_total = local * group
    pair = 2 * local

    digits = lax.div(me, 32), lax.rem(lax.div(me, 8), 4), lax.rem(lax.div(me, 2), 4), lax.rem(me, 2)
    layers = [lax.rem(digits[0] + near, 4) for near in range(4)]
    cores = [digits[3], 1 - digits[3]]

    def visit(outer, skip_self, act):
        y, x = digits[1] + lax.rem(outer, 4), digits[2] + lax.div(outer, 4)
        for near in range(4):
            column = lax.rem(y + near, 4) * 8 + lax.rem(x + near, 4) * 2
            side = lax.div(layers[near], 2)
            spot = layers[near] * 32 - side * group + column
            for core in range(2):
                if not (skip_self and near == 0 and core == 0):
                    act(side, spot + cores[core])

    def visit_others(act):
        visit(0, True, act)

        def one(outer, carry):
            visit(outer, False, act)
            return carry

        lax.fori_loop(1, devices // 8, one, 0)

    portion = local // GROUPS

    def spectrum_copy(g):
        some = pl.ds(g * portion, portion)
        return pltpu.make_async_copy(spectrum_hbm.at[some], total.at[some], spectrum_sem.at[g])

    def first_copy(g):
        some = pl.ds(g * portion, portion)
        return pltpu.make_async_copy(
            basis_hbm.at[some, pl.ds(0, rows), :], basis.at[0, some], first_sem.at[g]
        )

    for g in range(GROUPS):
        spectrum_copy(g).start()
        first_copy(g).start()

    scalar_copies = [
        pltpu.make_async_copy(source, target, scalar_sem.at[i])
        for i, (source, target) in enumerate(
            (
                (cutoff_hbm, cutoff),
                (couplings_hbm, couplings),
                (trap_hbm, trap),
                (weights_hbm, weights),
            )
        )
    ]
    for copy in scalar_copies:
        copy.start()

    def basis_copy(k):
        return pltpu.make_async_copy(
            basis_hbm.at[:, pl.ds(k * rows, rows), :], basis.at[k], basis_sem.at[k]
        )

    barrier = pltpu.get_barrier_semaphore()

    def greet(side, spot):
        pl.semaphore_signal(
            barrier, inc=1, device_id={"comp": side, "mr": spot}, device_id_type=MESH
        )

    visit_others(greet)
    tables_copy = pltpu.make_async_copy(tables_hbm, tables, load_sem)
    for k in range(1, CHUNKS):
        basis_copy(k).start()
    tables_copy.start()

    lane = lax.broadcasted_iota(jnp.int32, (1, 2 * planes), 1)
    first = lane < planes
    degree_ids = lax.broadcasted_iota(jnp.int32, (1, degrees), 1)

    mode_ids = place * local + lax.broadcasted_iota(jnp.int32, (local, 1), 0)
    signed = jnp.where(mode_ids < mode_total // 2, mode_ids, mode_ids - mode_total).astype(F32)
    energy = 2.0 * degree_ids.astype(F32) + (jnp.abs(signed) + 1.0 - ROTATION * signed)
    wave_sin[...], wave_cos[...] = sine_cosine(TIMESTEP * energy)

    def spin(m, carry):
        kept = jnp.where(degree_ids < cutoff[m], 1.0, 0.0)
        cosine, sine = wave_cos[pl.ds(m, 1), :] * kept, wave_sin[pl.ds(m, 1), :] * kept
        real, imag = total[m, 0:planes, :], total[m, planes:, :]
        coeffs[m, 0:planes, :] = (real * cosine + imag * sine).astype(BF16)
        coeffs[m, planes:, :] = (imag * cosine - real * sine).astype(BF16)
        return carry


    def swap_halves(low, high):
        return (
            jnp.where(first, low, pltpu.roll(high, planes, 1)),
            jnp.where(first, pltpu.roll(low, planes, 1), high),
        )

    def scatter(source, target, send, recv, k):
        def go(side, spot):
            pltpu.make_async_remote_copy(
                src_ref=source.at[k, side * group + spot],
                dst_ref=target.at[k, me],
                send_sem=send.at[k],
                recv_sem=recv.at[k],
                device_id={"comp": side, "mr": spot},
                device_id_type=MESH,
            ).start()

        visit_others(go)
        target[k, me] = source[k, me]

    def drain(buffer, sem, k):
        others = buffer.at[k, pl.ds(0, devices - 1)]
        pltpu.make_async_copy(others, others, sem.at[k]).wait()

    def one_mode(k, m):
        values = lax.dot_general(
            basis[k, m], coeffs[m], (((1,), (1,)), ((), ())), preferred_element_type=F32
        )
        real, imag = swap_halves(values[:half], values[half:])
        stage[pl.ds(m, devices, stride=pair), :] = real
        stage[pl.ds(local + m, devices, stride=pair), :] = imag

    def pack_all(k):
        def pack(b, carry):
            block = stage[pl.ds(pl.multiple_of(b * 8 * pair, 8 * pair), 8 * pair), :]
            sent[k, pl.ds(b * 8, 8)] = block.astype(BF16).reshape(8, pair, 2 * planes)
            return carry

        lax.fori_loop(0, devices // 8, pack, 0, unroll=2)

    def begin(g, carry):
        spectrum_copy(g).wait()
        for i in range(portion):
            spin(g * portion + i, 0)
        first_copy(g).wait()
        for i in range(portion):
            one_mode(0, g * portion + i)
        return carry

    for copy in scalar_copies:
        copy.wait()
    lax.fori_loop(0, GROUPS, begin, 0)
    pack_all(0)
    pl.semaphore_wait(barrier, devices - 1)
    scatter(sent, landed, send_sem, recv_sem, 0)

    def outward(k, carry):
        basis_copy(k).wait()

        def one(m, carry):
            one_mode(k, m)
            return carry

        lax.fori_loop(0, local, one, 0, unroll=4)
        pack_all(k)
        scatter(sent, landed, send_sem, recv_sem, k)
        return carry

    lax.fori_loop(1, CHUNKS, outward, 0)

    tables_copy.wait()
    low, high = pl.ds(0, quarter), pl.ds(quarter, quarter)
    for table, index, sign in ((forward, 0, 1), (inverse, 1, -1)):
        for s in range(QUARTERS):
            cosine, sine = tables[index, s, 0], tables[index, s, 1]
            table[s, low, low] = cosine
            table[s, high, high] = cosine
            table[s, high, low] = sine * sign
            table[s, low, high] = sine * -sign

    def physical(k):
        def radix_in(b, carry):
            for c in range(comps):
                x = []
                for h in range(QUARTERS):
                    tile = landed[k, c * group + h * quarter_places + b].astype(F32)
                    x.append((tile[:local], tile[local:]))
                (ar, ai), (br, bi) = [
                    (x[h][0] + x[h + 2][0], x[h][1] + x[h + 2][1]) for h in range(2)
                ]
                (er, ei), (fr, fi) = [
                    (x[h][0] - x[h + 2][0], x[h][1] - x[h + 2][1]) for h in range(2)
                ]
                mixed = (
                    (ar + br, ai + bi), (er - fi, ei + fr), (ar - br, ai - bi), (er + fi, ei - fr)
                )
                columns = pl.ds(c * 2 * planes, 2 * planes)
                start = pl.multiple_of(b * local, local)
                for s in range(QUARTERS):
                    turned[s, pl.ds(start, local), columns] = mixed[s][0].astype(BF16)
                    turned[s, pl.ds(quarter + start, local), columns] = mixed[s][1].astype(BF16)
            return carry

        lax.fori_loop(0, quarter_places, radix_in, 0, unroll=2)
        radius = k * rows + me
        scale = TIMESTEP / (2.0 * math.pi)
        own = [couplings[c, 0] * scale for c in range(comps)]
        other = [couplings[c, 1] * scale for c in range(comps)]
        potential = jnp.where(first, trap[radius], trap[radius + half]) * scale
        measure = jnp.where(first, weights[radius], weights[radius + half])

        def transform(s, carry):
            field[...] = jnp.dot(forward[s], turned[s], preferred_element_type=F32)

            def kick(b, carry):
                start = pl.multiple_of(b * 32, 32)
                psi = []
                for c in range(comps):
                    columns = pl.ds(c * 2 * planes, 2 * planes)
                    psi.append(
                        (field[pl.ds(start, 32), columns], field[pl.ds(quarter + start, 32), columns])
                    )
                density = [real * real + imag * imag for real, imag in psi]
                for c in range(comps):
                    columns = pl.ds(c * 2 * planes, 2 * planes)
                    turns = own[c] * density[c] + other[c] * density[1 - c] + potential
                    sine, cosine = sine_cosine_of_turns(turns)
                    real, imag = psi[c]
                    kicked[pl.ds(start, 32), columns] = (real * cosine + imag * sine).astype(BF16)
                    kicked[pl.ds(quarter + start, 32), columns] = (
                        imag * cosine - real * sine
                    ).astype(BF16)
                return carry

            lax.fori_loop(0, quarter // 32, kick, 0, unroll=2)
            modes[s] = jnp.dot(inverse[s], kicked[...], preferred_element_type=F32)
            return carry

        lax.fori_loop(0, QUARTERS, transform, 0)

        def radix_out(b, carry):
            start = pl.multiple_of(b * local, local)
            for c in range(comps):
                columns = pl.ds(c * 2 * planes, 2 * planes)
                x = [
                    (
                        modes[s, pl.ds(start, local), columns],
                        modes[s, pl.ds(quarter + start, local), columns],
                    )
                    for s in range(QUARTERS)
                ]
                (ar, ai), (br, bi) = [
                    (x[h][0] + x[h + 2][0], x[h][1] + x[h + 2][1]) for h in range(2)
                ]
                (er, ei), (fr, fi) = [
                    (x[h][0] - x[h + 2][0], x[h][1] - x[h + 2][1]) for h in range(2)
                ]
                mixed = (
                    (ar + br, ai + bi), (er + fi, ei - fr), (ar - br, ai - bi), (er - fi, ei + fr)
                )
                for h in range(QUARTERS):
                    device = c * group + h * quarter_places + b
                    sent_back[k, device, 0:local, :] = (mixed[h][0] * measure).astype(BF16)
                    sent_back[k, device, local:, :] = (mixed[h][1] * measure).astype(BF16)
            return carry

        lax.fori_loop(0, quarter_places, radix_out, 0, unroll=2)

    def analyze(k, starts, last):
        drain(landed_back, recv_back_sem, k)

        def unpack(b, carry):
            block = landed_back[k, pl.ds(b * 8, 8)].astype(F32)
            stage[pl.ds(pl.multiple_of(b * 8 * pair, 8 * pair), 8 * pair), :] = block.reshape(
                8 * pair, 2 * planes
            )
            return carry

        lax.fori_loop(0, devices // 8, unpack, 0, unroll=2)

        def one(m, carry):
            parts = []
            for p in range(2):
                block = stage[pl.ds(p * local + m, devices, stride=pair), :].T.astype(BF16)
                parts.append(jnp.concatenate([block[:planes], block[planes:]], 1))
            values = jnp.dot(jnp.concatenate(parts, 0), basis[k, m], preferred_element_type=F32)
            if not starts:
                values = total[m] + values
            if last:
                values = values * jnp.where(degree_ids < cutoff[m], 1.0, 0.0)
            total[m] = values
            return carry

        lax.fori_loop(0, local, one, 0, unroll=4)

    def back(k, carry):
        drain(landed, recv_sem, k)
        physical(k)
        scatter(sent_back, landed_back, send_back_sem, recv_back_sem, k)
        return carry

    def gather(k, carry):
        analyze(k, False, False)
        return carry

    lax.fori_loop(0, CHUNKS, back, 0)
    analyze(0, True, False)
    lax.fori_loop(1, CHUNKS - 1, gather, 0)
    analyze(CHUNKS - 1, False, True)

    def finish(k, carry):
        drain(sent, send_sem, k)
        drain(sent_back, send_back_sem, k)
        return carry

    lax.fori_loop(0, CHUNKS, finish, 0)


def on_device(spectrum, radial_basis, cutoff, couplings, trap_potential, weights):
    local_modes, _, planes, degrees = spectrum.shape[1:]
    radius_count = radial_basis.shape[1]
    devices = lax.axis_size("comp") * lax.axis_size("mr")
    mode_total = local_modes * lax.axis_size("mr")
    rows = radius_count // CHUNKS
    width = 2 * planes
    quarter = mode_total // QUARTERS
    pair = 2 * local_modes
    comps = lax.axis_size("comp")
    blocks = pltpu.VMEM((CHUNKS, devices, pair, width), BF16)
    outside = pl.BlockSpec(memory_space=pltpu.HBM)
    evolved = pl.pallas_call(
        kernel,
        out_shape=jax.ShapeDtypeStruct((local_modes, width, degrees), F32),
        in_specs=[outside] * 7,
        out_specs=pl.BlockSpec(memory_space=pltpu.VMEM),
        scratch_shapes=[
            pltpu.VMEM((CHUNKS, local_modes, rows, degrees), BF16),
            pltpu.VMEM((local_modes, width, degrees), BF16),
            pltpu.VMEM((2, QUARTERS, 2, quarter, quarter), BF16),
            pltpu.VMEM((QUARTERS, 2 * quarter, 2 * quarter), BF16),
            pltpu.VMEM((QUARTERS, 2 * quarter, 2 * quarter), BF16),
            blocks,
            blocks,
            blocks,
            blocks,
            pltpu.VMEM((devices * pair, width), F32),
            pltpu.VMEM((QUARTERS, 2 * quarter, comps * width), BF16),
            pltpu.VMEM((2 * quarter, comps * width), F32),
            pltpu.VMEM((2 * quarter, comps * width), BF16),
            pltpu.VMEM((QUARTERS, 2 * quarter, comps * width), F32),
            pltpu.VMEM((local_modes, degrees), F32),
            pltpu.VMEM((local_modes, degrees), F32),
            pltpu.SMEM((local_modes,), jnp.int32),
            pltpu.SMEM((comps, comps), F32),
            pltpu.SMEM((radius_count,), F32),
            pltpu.SMEM((radius_count,), F32),
            pltpu.SemaphoreType.DMA,
            pltpu.SemaphoreType.DMA((4,)),
            pltpu.SemaphoreType.DMA((GROUPS,)),
            pltpu.SemaphoreType.DMA((GROUPS,)),
            pltpu.SemaphoreType.DMA((CHUNKS,)),
            pltpu.SemaphoreType.DMA((CHUNKS,)),
            pltpu.SemaphoreType.DMA((CHUNKS,)),
            pltpu.SemaphoreType.DMA((CHUNKS,)),
            pltpu.SemaphoreType.DMA((CHUNKS,)),
        ],
        compiler_params=pltpu.CompilerParams(collective_id=0, has_side_effects=True, vmem_limit_bytes=47 << 20),
    )(
        *[
            pltpu.with_memory_space_constraint(x, pltpu.HBM)
            for x in (
                cutoff,
                couplings,
                trap_potential,
                weights,
                spectrum.reshape(local_modes, width, degrees),
                radial_basis,
                jnp.asarray(quarter_tables(mode_total)),
            )
        ]
    )
    return evolved.reshape(1, local_modes, 2, planes, degrees)


def solution(mesh):
    in_specs = (P("comp", "mr", None, None, None), P("mr", None, None), P("mr"), P(), P(), P())
    out_specs = P("comp", "mr", None, None, None)
    return jax.shard_map(
        on_device, mesh=mesh, in_specs=in_specs, out_specs=out_specs, check_vma=False
    )
```

```python
import functools
import math

import jax
import jax.numpy as jnp
import ml_dtypes
import numpy as np
from jax import lax
from jax.experimental import pallas as pl
from jax.experimental.pallas import tpu as pltpu
from jax.sharding import PartitionSpec as P

TIMESTEP = 0.5
ROTATION = 0.7
MESH = pl.DeviceIdType.MESH
CHUNKS = 4
GROUPS = 4
QUARTERS = 4
F32 = jnp.float32
BF16 = jnp.bfloat16


def quarter_tables(mode_total):
    quarter = mode_total // QUARTERS
    angle = QUARTERS * np.arange(quarter)[None, :, None] + np.arange(QUARTERS)[:, None, None]
    product = angle * np.arange(quarter)[None, None, :] % mode_total
    turn = product * (2.0 * math.pi / mode_total)
    both = np.stack([np.cos(turn), np.sin(turn)], 1) / math.sqrt(mode_total)
    both = both.astype(np.float32).astype(ml_dtypes.bfloat16)
    return np.stack([both, both.swapaxes(-1, -2)])


def sine_cosine(angle):
    turns = jnp.round(angle * (2.0 / math.pi))
    rest = angle - turns * 1.5703125
    rest = rest - turns * 4.837512969970703125e-4
    rest = rest - turns * 7.54978995489188e-8
    rest = jnp.clip(rest, -0.8, 0.8)
    square = rest * rest
    sine = ((-1.9515295891e-4 * square + 8.3321608736e-3) * square - 1.6666654611e-1) * square
    sine = sine * rest + rest
    cosine = (2.443315711809948e-5 * square - 1.388731625493765e-3) * square
    cosine = (cosine + 4.166664568298827e-2) * square * square - 0.5 * square + 1.0
    corner = (turns - 4.0 * jnp.floor(turns * 0.25)).astype(jnp.int32)
    swap = (corner & 1) == 1
    sine, cosine = jnp.where(swap, cosine, sine), jnp.where(swap, sine, cosine)
    sine = jnp.where(corner >= 2, -sine, sine)
    cosine = jnp.where((corner == 1) | (corner == 2), -cosine, cosine)
    return sine, cosine


def sine_cosine_of_turns(turns):
    rest = turns - jnp.round(turns)
    square = rest * rest
    twice = 0.1553153206018442 * square - 1.1965825712357152
    twice = (twice * square + 5.100155046428268) * square - 10.335420167015725
    twice = (twice * square + 6.283185280261414) * rest
    cosine = 0.2196896110917421 * square - 1.3318765680776314
    cosine = (cosine * square + 4.058411352862034) * square - 4.93479283061961
    cosine = cosine * square + 0.9999999532476082
    return twice * cosine, 1.0 - 0.5 * (twice * twice)


def kernel(
    cutoff_hbm, couplings_hbm, trap_hbm, weights_hbm, spectrum_hbm, basis_hbm, tables_hbm, total,
    basis, coeffs, tables, forward, inverse, sent, landed, sent_back, landed_back,
    stage, turned, field, kicked, modes, wave_cos, wave_sin,
    cutoff, couplings, trap, weights, load_sem, scalar_sem, spectrum_sem, first_sem, basis_sem, send_sem, recv_sem, send_back_sem, recv_back_sem,
):
    comps, group = lax.axis_size("comp"), lax.axis_size("mr")
    comp, place = lax.axis_index("comp"), lax.axis_index("mr")
    devices = comps * group
    me = comp * group + place
    local = coeffs.shape[0]
    planes = coeffs.shape[1] // 2
    degrees = coeffs.shape[2]
    rows = basis.shape[2]
    half = rows // 2
    quarter = forward.shape[1] // 2
    quarter_places = group // QUARTERS
    mode_total = local * group
    pair = 2 * local

    digits = lax.div(me, 32), lax.rem(lax.div(me, 8), 4), lax.rem(lax.div(me, 2), 4), lax.rem(me, 2)
    layers = [lax.rem(digits[0] + near, 4) for near in range(4)]
    cores = [digits[3], 1 - digits[3]]

    def visit(outer, skip_self, act):
        y, x = digits[1] + lax.rem(outer, 4), digits[2] + lax.div(outer, 4)
        for near in range(4):
            column = lax.rem(y + near, 4) * 8 + lax.rem(x + near, 4) * 2
            side = lax.div(layers[near], 2)
            spot = layers[near] * 32 - side * group + column
            for core in range(2):
                if not (skip_self and near == 0 and core == 0):
                    act(side, spot + cores[core])

    def visit_others(act):
        visit(0, True, act)

        def one(outer, carry):
            visit(outer, False, act)
            return carry

        lax.fori_loop(1, devices // 8, one, 0)

    portion = local // GROUPS

    def spectrum_copy(g):
        some = pl.ds(g * portion, portion)
        return pltpu.make_async_copy(spectrum_hbm.at[some], total.at[some], spectrum_sem.at[g])

    def first_copy(g):
        some = pl.ds(g * portion, portion)
        return pltpu.make_async_copy(
            basis_hbm.at[some, pl.ds(0, rows), :], basis.at[0, some], first_sem.at[g]
        )

    for g in range(GROUPS):
        spectrum_copy(g).start()
        first_copy(g).start()

    scalar_copies = [
        pltpu.make_async_copy(source, target, scalar_sem.at[i])
        for i, (source, target) in enumerate(
            (
                (cutoff_hbm, cutoff),
                (couplings_hbm, couplings),
                (trap_hbm, trap),
                (weights_hbm, weights),
            )
        )
    ]
    for copy in scalar_copies:
        copy.start()

    def basis_copy(k):
        return pltpu.make_async_copy(
            basis_hbm.at[:, pl.ds(k * rows, rows), :], basis.at[k], basis_sem.at[k]
        )

    barrier = pltpu.get_barrier_semaphore()

    def greet(side, spot):
        pl.semaphore_signal(
            barrier, inc=1, device_id={"comp": side, "mr": spot}, device_id_type=MESH
        )

    visit_others(greet)
    tables_copy = pltpu.make_async_copy(tables_hbm, tables, load_sem)
    for k in range(1, CHUNKS):
        basis_copy(k).start()
    tables_copy.start()

    lane = lax.broadcasted_iota(jnp.int32, (1, 2 * planes), 1)
    first = lane < planes
    degree_ids = lax.broadcasted_iota(jnp.int32, (1, degrees), 1)

    mode_ids = place * local + lax.broadcasted_iota(jnp.int32, (local, 1), 0)
    signed = jnp.where(mode_ids < mode_total // 2, mode_ids, mode_ids - mode_total).astype(F32)
    energy = 2.0 * degree_ids.astype(F32) + (jnp.abs(signed) + 1.0 - ROTATION * signed)
    wave_sin[...], wave_cos[...] = sine_cosine(TIMESTEP * energy)

    def spin(m, carry):
        kept = jnp.where(degree_ids < cutoff[m], 1.0, 0.0)
        cosine, sine = wave_cos[pl.ds(m, 1), :] * kept, wave_sin[pl.ds(m, 1), :] * kept
        real, imag = total[m, 0:planes, :], total[m, planes:, :]
        coeffs[m, 0:planes, :] = (real * cosine + imag * sine).astype(BF16)
        coeffs[m, planes:, :] = (imag * cosine - real * sine).astype(BF16)
        return carry


    def swap_halves(low, high):
        return (
            jnp.where(first, low, pltpu.roll(high, planes, 1)),
            jnp.where(first, pltpu.roll(low, planes, 1), high),
        )

    def scatter(source, target, send, recv, k):
        def go(side, spot):
            pltpu.make_async_remote_copy(
                src_ref=source.at[k, side * group + spot],
                dst_ref=target.at[k, me],
                send_sem=send.at[k],
                recv_sem=recv.at[k],
                device_id={"comp": side, "mr": spot},
                device_id_type=MESH,
            ).start()

        visit_others(go)
        target[k, me] = source[k, me]

    def drain(buffer, sem, k):
        others = buffer.at[k, pl.ds(0, devices - 1)]
        pltpu.make_async_copy(others, others, sem.at[k]).wait()

    def one_mode(k, m):
        values = lax.dot_general(
            basis[k, m], coeffs[m], (((1,), (1,)), ((), ())), preferred_element_type=F32
        )
        real, imag = swap_halves(values[:half], values[half:])
        stage[pl.ds(m, devices, stride=pair), :] = real
        stage[pl.ds(local + m, devices, stride=pair), :] = imag

    def pack_all(k):
        def pack(b, carry):
            block = stage[pl.ds(pl.multiple_of(b * 8 * pair, 8 * pair), 8 * pair), :]
            sent[k, pl.ds(b * 8, 8)] = block.astype(BF16).reshape(8, pair, 2 * planes)
            return carry

        lax.fori_loop(0, devices // 8, pack, 0, unroll=2)

    def begin(g, carry):
        spectrum_copy(g).wait()
        for i in range(portion):
            spin(g * portion + i, 0)
        first_copy(g).wait()
        for i in range(portion):
            one_mode(0, g * portion + i)
        return carry

    for copy in scalar_copies:
        copy.wait()
    lax.fori_loop(0, GROUPS, begin, 0)
    pack_all(0)
    pl.semaphore_wait(barrier, devices - 1)
    scatter(sent, landed, send_sem, recv_sem, 0)

    def outward(k, carry):
        basis_copy(k).wait()

        def one(m, carry):
            one_mode(k, m)
            return carry

        lax.fori_loop(0, local, one, 0, unroll=8)
        pack_all(k)
        scatter(sent, landed, send_sem, recv_sem, k)
        return carry

    lax.fori_loop(1, CHUNKS, outward, 0)

    tables_copy.wait()
    low, high = pl.ds(0, quarter), pl.ds(quarter, quarter)
    for table, index, sign in ((forward, 0, 1), (inverse, 1, -1)):
        for s in range(QUARTERS):
            cosine, sine = tables[index, s, 0], tables[index, s, 1]
            table[s, low, low] = cosine
            table[s, high, high] = cosine
            table[s, high, low] = sine * sign
            table[s, low, high] = sine * -sign

    def physical(k):
        def radix_in(b, carry):
            for c in range(comps):
                x = []
                for h in range(QUARTERS):
                    tile = landed[k, c * group + h * quarter_places + b].astype(F32)
                    x.append((tile[:local], tile[local:]))
                (ar, ai), (br, bi) = [
                    (x[h][0] + x[h + 2][0], x[h][1] + x[h + 2][1]) for h in range(2)
                ]
                (er, ei), (fr, fi) = [
                    (x[h][0] - x[h + 2][0], x[h][1] - x[h + 2][1]) for h in range(2)
                ]
                mixed = (
                    (ar + br, ai + bi), (er - fi, ei + fr), (ar - br, ai - bi), (er + fi, ei - fr)
                )
                columns = pl.ds(c * 2 * planes, 2 * planes)
                start = pl.multiple_of(b * local, local)
                for s in range(QUARTERS):
                    turned[s, pl.ds(start, local), columns] = mixed[s][0].astype(BF16)
                    turned[s, pl.ds(quarter + start, local), columns] = mixed[s][1].astype(BF16)
            return carry

        lax.fori_loop(0, quarter_places, radix_in, 0, unroll=2)
        radius = k * rows + me
        scale = TIMESTEP / (2.0 * math.pi)
        own = [couplings[c, 0] * scale for c in range(comps)]
        other = [couplings[c, 1] * scale for c in range(comps)]
        potential = jnp.where(first, trap[radius], trap[radius + half]) * scale
        measure = jnp.where(first, weights[radius], weights[radius + half])

        def transform(s, carry):
            field[...] = jnp.dot(forward[s], turned[s], preferred_element_type=F32)

            def kick(b, carry):
                start = pl.multiple_of(b * 32, 32)
                psi = []
                for c in range(comps):
                    columns = pl.ds(c * 2 * planes, 2 * planes)
                    psi.append(
                        (field[pl.ds(start, 32), columns], field[pl.ds(quarter + start, 32), columns])
                    )
                density = [real * real + imag * imag for real, imag in psi]
                for c in range(comps):
                    columns = pl.ds(c * 2 * planes, 2 * planes)
                    turns = own[c] * density[c] + other[c] * density[1 - c] + potential
                    sine, cosine = sine_cosine_of_turns(turns)
                    real, imag = psi[c]
                    kicked[pl.ds(start, 32), columns] = (real * cosine + imag * sine).astype(BF16)
                    kicked[pl.ds(quarter + start, 32), columns] = (
                        imag * cosine - real * sine
                    ).astype(BF16)
                return carry

            lax.fori_loop(0, quarter // 32, kick, 0, unroll=2)
            modes[s] = jnp.dot(inverse[s], kicked[...], preferred_element_type=F32)
            return carry

        lax.fori_loop(0, QUARTERS, transform, 0)

        def radix_out(b, carry):
            start = pl.multiple_of(b * local, local)
            for c in range(comps):
                columns = pl.ds(c * 2 * planes, 2 * planes)
                x = [
                    (
                        modes[s, pl.ds(start, local), columns],
                        modes[s, pl.ds(quarter + start, local), columns],
                    )
                    for s in range(QUARTERS)
                ]
                (ar, ai), (br, bi) = [
                    (x[h][0] + x[h + 2][0], x[h][1] + x[h + 2][1]) for h in range(2)
                ]
                (er, ei), (fr, fi) = [
                    (x[h][0] - x[h + 2][0], x[h][1] - x[h + 2][1]) for h in range(2)
                ]
                mixed = (
                    (ar + br, ai + bi), (er + fi, ei - fr), (ar - br, ai - bi), (er - fi, ei + fr)
                )
                for h in range(QUARTERS):
                    device = c * group + h * quarter_places + b
                    sent_back[k, device, 0:local, :] = (mixed[h][0] * measure).astype(BF16)
                    sent_back[k, device, local:, :] = (mixed[h][1] * measure).astype(BF16)
            return carry

        lax.fori_loop(0, quarter_places, radix_out, 0, unroll=2)

    def analyze(k, starts, last):
        drain(landed_back, recv_back_sem, k)

        def unpack(b, carry):
            block = landed_back[k, pl.ds(b * 8, 8)].astype(F32)
            stage[pl.ds(pl.multiple_of(b * 8 * pair, 8 * pair), 8 * pair), :] = block.reshape(
                8 * pair, 2 * planes
            )
            return carry

        lax.fori_loop(0, devices // 8, unpack, 0, unroll=2)

        def one(m, carry):
            parts = []
            for p in range(2):
                block = stage[pl.ds(p * local + m, devices, stride=pair), :].T.astype(BF16)
                parts.append(jnp.concatenate([block[:planes], block[planes:]], 1))
            values = jnp.dot(jnp.concatenate(parts, 0), basis[k, m], preferred_element_type=F32)
            if not starts:
                values = total[m] + values
            if last:
                values = values * jnp.where(degree_ids < cutoff[m], 1.0, 0.0)
            total[m] = values
            return carry

        lax.fori_loop(0, local, one, 0, unroll=8)

    def back(k, carry):
        drain(landed, recv_sem, k)
        physical(k)
        scatter(sent_back, landed_back, send_back_sem, recv_back_sem, k)
        return carry

    def gather(k, carry):
        analyze(k, False, False)
        return carry

    lax.fori_loop(0, CHUNKS, back, 0)
    analyze(0, True, False)
    lax.fori_loop(1, CHUNKS - 1, gather, 0)
    analyze(CHUNKS - 1, False, True)

    def finish(k, carry):
        drain(sent, send_sem, k)
        drain(sent_back, send_back_sem, k)
        return carry

    lax.fori_loop(0, CHUNKS, finish, 0)


def on_device(spectrum, radial_basis, cutoff, couplings, trap_potential, weights):
    local_modes, _, planes, degrees = spectrum.shape[1:]
    radius_count = radial_basis.shape[1]
    devices = lax.axis_size("comp") * lax.axis_size("mr")
    mode_total = local_modes * lax.axis_size("mr")
    rows = radius_count // CHUNKS
    width = 2 * planes
    quarter = mode_total // QUARTERS
    pair = 2 * local_modes
    comps = lax.axis_size("comp")
    blocks = pltpu.VMEM((CHUNKS, devices, pair, width), BF16)
    outside = pl.BlockSpec(memory_space=pltpu.HBM)
    evolved = pl.pallas_call(
        kernel,
        out_shape=jax.ShapeDtypeStruct((local_modes, width, degrees), F32),
        in_specs=[outside] * 7,
        out_specs=pl.BlockSpec(memory_space=pltpu.VMEM),
        scratch_shapes=[
            pltpu.VMEM((CHUNKS, local_modes, rows, degrees), BF16),
            pltpu.VMEM((local_modes, width, degrees), BF16),
            pltpu.VMEM((2, QUARTERS, 2, quarter, quarter), BF16),
            pltpu.VMEM((QUARTERS, 2 * quarter, 2 * quarter), BF16),
            pltpu.VMEM((QUARTERS, 2 * quarter, 2 * quarter), BF16),
            blocks,
            blocks,
            blocks,
            blocks,
            pltpu.VMEM((devices * pair, width), F32),
            pltpu.VMEM((QUARTERS, 2 * quarter, comps * width), BF16),
            pltpu.VMEM((2 * quarter, comps * width), F32),
            pltpu.VMEM((2 * quarter, comps * width), BF16),
            pltpu.VMEM((QUARTERS, 2 * quarter, comps * width), F32),
            pltpu.VMEM((local_modes, degrees), F32),
            pltpu.VMEM((local_modes, degrees), F32),
            pltpu.SMEM((local_modes,), jnp.int32),
            pltpu.SMEM((comps, comps), F32),
            pltpu.SMEM((radius_count,), F32),
            pltpu.SMEM((radius_count,), F32),
            pltpu.SemaphoreType.DMA,
            pltpu.SemaphoreType.DMA((4,)),
            pltpu.SemaphoreType.DMA((GROUPS,)),
            pltpu.SemaphoreType.DMA((GROUPS,)),
            pltpu.SemaphoreType.DMA((CHUNKS,)),
            pltpu.SemaphoreType.DMA((CHUNKS,)),
            pltpu.SemaphoreType.DMA((CHUNKS,)),
            pltpu.SemaphoreType.DMA((CHUNKS,)),
            pltpu.SemaphoreType.DMA((CHUNKS,)),
        ],
        compiler_params=pltpu.CompilerParams(collective_id=0, has_side_effects=True, vmem_limit_bytes=47 << 20),
    )(
        *[
            pltpu.with_memory_space_constraint(x, pltpu.HBM)
            for x in (
                cutoff,
                couplings,
                trap_potential,
                weights,
                spectrum.reshape(local_modes, width, degrees),
                radial_basis,
                jnp.asarray(quarter_tables(mode_total)),
            )
        ]
    )
    return evolved.reshape(1, local_modes, 2, planes, degrees)


def solution(mesh):
    in_specs = (P("comp", "mr", None, None, None), P("mr", None, None), P("mr"), P(), P(), P())
    out_specs = P("comp", "mr", None, None, None)
    return jax.shard_map(
        on_device, mesh=mesh, in_specs=in_specs, out_specs=out_specs, check_vma=False
    )
```
